32 devices in a mesh: seq: 8 (over z, y), ch: 4 (over x, core).
Axes of the slice: x: 2, y: 2, z: 4, core: 2. Of those that a mesh axis runs over, the one named last changes fastest.
Arguments:
- mamba_in: bfloat16 [2048, 8192], P('seq', 'ch'), may hold values from -6 to 6
- gate_in: bfloat16 [2048, 8192], P('seq', 'ch'), may hold values from -6 to 6
- delta_in: bfloat16 [2048, 8192], P('seq', 'ch'), may hold values from -3 to 16
- step_bias: float32 [8192], P('ch'), may hold values from -12 to 1.5
- decay_log: float32 [8192, 16], P('ch'), may hold values from -3.9 to -1.6
- input_map_state: bfloat16 [2048, 16], P('seq'), may hold values from -6 to 6
- state_out: bfloat16 [2048, 16], P('seq'), may hold values from -1.5 to 1.5
- skip_gain: float32 [8192], P('ch'), may hold values from 0.5 to 1.5
- out_weight: bfloat16 [8192, 8192], P('ch'), may hold values from -0.0625 to 0.0625
- residual: bfloat16 [2048, 8192], P('seq', 'ch'), may hold values from -6 to 6
- norm_gain: bfloat16 [8192], P('ch'), may hold values from 0.5 to 1.5
- query_weight: bfloat16 [8192, 8192], P('seq', 'ch'), may hold values from -1 to 1
- key_weight: bfloat16 [8192, 1024], P('seq'), may hold values from -1 to 1
- value_weight: bfloat16 [8192, 1024], P('seq'), may hold values from -0.0625 to 0.0625
Outputs:
- mamba_out: bfloat16 [2048, 8192], P('seq', 'ch')
- attention_out: bfloat16 [2048, 8192], P('seq', 'ch')
The draws below stay inside these ranges and needn't reach their ends.
All inputs are finite; a program needn't handle non-finite values.
Results may differ from the reference program's by a relative error of at most 0.01.
Values may be sent and summed in bfloat16 or wider, within the bound.
No kernel may reach another device: no remote copies, remote signals or barrier semaphores. Data moves between devices by JAX's collectives and lax.ppermute only.
A program may use at most 128 MiB of HBM per device.

```python
import math
from functools import partial
import jax
import jax.numpy as jnp
from jax import lax

D = 8192
MCH = 8192
H = 64
KVH = 8
HD = 128
NSTATE = 16
TOKENS = 2048


def draw_delta_in(key, part):
    base_key = jax.random.fold_in(key, 11)
    base_offset = jnp.clip(0.5 * jax.random.normal(base_key, (TOKENS, MCH), jnp.float32), -3.0, 3.0)
    slot_indices = jax.random.randint(jax.random.fold_in(key, 12), (3,), 0, TOKENS)
    token_positions = jnp.arange(TOKENS)
    token_group = jnp.any(token_positions[:, None] == slot_indices[None, :], axis=1)
    return (base_offset + jnp.where(token_group, 13.0, 0.0)[:, None]).astype(jnp.bfloat16)


def draw_step_bias(key, part):
    slow = jax.random.randint(jax.random.fold_in(key, 31), (MCH,), 0, 2) > 0
    slow_step = jax.random.uniform(jax.random.fold_in(key, 32), (MCH,), jnp.float32, 0.1, 0.5) / (0.2 * TOKENS)
    fast_step = jax.random.uniform(jax.random.fold_in(key, 33), (MCH,), jnp.float32, 0.3, 1.5)
    chosen = jnp.where(slow, slow_step, fast_step)
    return jnp.log(jnp.expm1(chosen)).astype(jnp.float32)


def shared_keys(key):
    return jax.random.normal(jax.random.fold_in(key, 21), (D, KVH * HD), jnp.float32) / math.sqrt(D)


def draw_key_weight(key, part):
    return jnp.clip(shared_keys(key), -1.0, 1.0).astype(jnp.bfloat16)


def draw_query_weight(key, part):
    own_part = jax.random.normal(jax.random.fold_in(key, 22), (D, H * HD), jnp.float32) / math.sqrt(D)
    return jnp.clip(own_part, -1.0, 1.0).astype(jnp.bfloat16)


def block_levels(rng, shape, shards, smallest, largest):
    factor_of, own = 1.0, jax.random.fold_in(rng, 6)
    for position, parts in shards:
        heights = jnp.exp(jax.random.uniform(jax.random.fold_in(own, position), (parts,), jnp.float32, smallest / len(shards), largest / len(shards)))
        factor_of = factor_of * jnp.repeat(heights, shape[position] // parts).reshape([-1 if axis == position else 1 for axis in range(len(shape))])
    return factor_of


def normal_values(key, extent, scale, reach, shards=(), kind=jnp.bfloat16):
    values = scale * jax.random.normal(key, extent, jnp.float32)
    if shards:
        values = values * block_levels(key, extent, shards, -0.22, 0.18)
    return jnp.clip(values, -reach, reach).astype(kind)


def setup_inputs(seed: int = 0) -> dict:
    arg_keys = jax.random.split(jax.random.key(seed), 15)
    mamba_in = normal_values(arg_keys[0], (TOKENS, MCH), 1.0, 6.0, ((0, 8), (1, 4)))
    gate_in = normal_values(arg_keys[1], (TOKENS, MCH), 1.0, 6.0, ((0, 8), (1, 4)))
    delta_in = draw_delta_in(jax.random.fold_in(arg_keys[14], 71), 0)
    step_bias = draw_step_bias(jax.random.fold_in(arg_keys[14], 71), 0)
    decay_log = jnp.clip(-3.9 + 2.3000001 * jax.random.uniform(arg_keys[4], (MCH, NSTATE), jnp.float32) ** block_levels(arg_keys[4], (MCH, NSTATE), ((0, 4),), -0.2, 0.2), -3.9, -1.6)
    input_map_state = normal_values(arg_keys[5], (TOKENS, NSTATE), 1.0, 6.0, ((0, 8),))
    state_out = normal_values(arg_keys[6], (TOKENS, NSTATE), NSTATE ** -0.5, 1.5, ((0, 8),))
    skip_gain = jnp.clip(0.5 + 1.0 * jax.random.uniform(arg_keys[7], (MCH,), jnp.float32) ** block_levels(arg_keys[7], (MCH,), ((0, 4),), -0.2, 0.2), 0.5, 1.5)
    out_weight = normal_values(arg_keys[8], (MCH, D), MCH ** -0.5, 0.0625, ((0, 4),))
    residual = normal_values(arg_keys[9], (TOKENS, D), 1.0, 6.0, ((0, 8), (1, 4)))
    norm_gain = jnp.clip(1.0 + 0.1 * jax.random.normal(arg_keys[10], (D,), jnp.float32), 0.5, 1.5).astype(jnp.bfloat16)
    query_weight = draw_query_weight(jax.random.fold_in(arg_keys[14], 71), 0)
    key_weight = draw_key_weight(jax.random.fold_in(arg_keys[14], 71), 0)
    value_weight = normal_values(arg_keys[13], (D, KVH * HD), D ** -0.5, 0.0625, ((0, 8),))
    return dict(mamba_in=mamba_in, gate_in=gate_in, delta_in=delta_in, step_bias=step_bias, decay_log=decay_log, input_map_state=input_map_state, state_out=state_out, skip_gain=skip_gain, out_weight=out_weight, residual=residual, norm_gain=norm_gain, query_weight=query_weight, key_weight=key_weight, value_weight=value_weight)


def head_output(queries, keys_all, values_all, head):
    group_size = H // KVH
    query_cols = lax.dynamic_slice_in_dim(queries, head * HD, HD, 1)
    kv_index = head // group_size
    key_cols = lax.dynamic_slice_in_dim(keys_all, kv_index * HD, HD, 1)
    value_cols = lax.dynamic_slice_in_dim(values_all, kv_index * HD, HD, 1)
    scores = jnp.dot(query_cols, key_cols.T, preferred_element_type=jnp.float32) * (1.0 / math.sqrt(HD))
    token_positions = jnp.arange(TOKENS, dtype=jnp.int32)
    allowed = token_positions[None, :] <= token_positions[:, None]
    scores = jnp.where(allowed, scores, -1e+30)
    highest = lax.optimization_barrier(jnp.max(scores, axis=1, keepdims=True))
    weights = jnp.where(allowed, jnp.exp(scores - highest), 0.0)
    numer = jnp.dot(weights.astype(jnp.bfloat16), value_cols, preferred_element_type=jnp.float32)
    return numer / lax.optimization_barrier(jnp.sum(weights, axis=1, keepdims=True))

def reference(mamba_in, gate_in, delta_in, step_bias, decay_log, input_map_state, state_out, skip_gain, out_weight, residual, norm_gain, query_weight, key_weight, value_weight):
    decay_rate = jnp.exp(decay_log)
    step_size = jax.nn.softplus(delta_in.astype(jnp.float32) + step_bias)
    drive_rows = mamba_in.astype(jnp.float32)

    def advance(carried_state, inputs):
        step_row, drive_row, input_row, output_row = inputs
        carried_state = jnp.exp(-step_row[:, None] * decay_rate) * carried_state + (step_row * drive_row)[:, None] * input_row[None, :]
        return (carried_state, lax.optimization_barrier(jnp.sum(carried_state * output_row[None, :], axis=1)))
    _, local_out = lax.scan(advance, jnp.zeros((MCH, NSTATE), jnp.float32), (step_size, drive_rows, input_map_state.astype(jnp.float32), state_out.astype(jnp.float32)))
    scanned = local_out + skip_gain * drive_rows
    gated = (scanned * jax.nn.silu(gate_in.astype(jnp.float32))).astype(jnp.bfloat16)
    projected = jnp.dot(gated, out_weight, preferred_element_type=jnp.float32)
    mamba_out = (residual.astype(jnp.float32) + projected).astype(jnp.bfloat16)
    mixed_rows = mamba_out.astype(jnp.float32)
    meansq = lax.optimization_barrier(jnp.mean(jnp.square(mixed_rows), axis=1, keepdims=True))
    normed = (mixed_rows * lax.rsqrt(meansq + 1e-06) * norm_gain.astype(jnp.float32)).astype(jnp.bfloat16)
    queries = jnp.dot(normed, query_weight, preferred_element_type=jnp.float32).astype(jnp.bfloat16)
    keys_all = jnp.dot(normed, key_weight, preferred_element_type=jnp.float32).astype(jnp.bfloat16)
    values_all = jnp.dot(normed, value_weight, preferred_element_type=jnp.float32).astype(jnp.bfloat16)
    heads = lax.map(partial(head_output, queries, keys_all, values_all), jnp.arange(H, dtype=jnp.int32))
    attention_out = jnp.transpose(heads, (1, 0, 2)).reshape(TOKENS, H * HD).astype(jnp.bfloat16)
    return (mamba_out, attention_out)
```

```python
import math

import jax
import jax.numpy as jnp
from jax import lax
from jax.experimental import pallas as pl
from jax.experimental.pallas import tpu as pltpu
from jax.sharding import PartitionSpec as P


HD = 128
LOG2E = 1.4426950408889634
F32 = jnp.float32
BF16 = jnp.bfloat16
Q_PIECES = 4


def cost(flops, bytes_moved, exps=0):
    return pl.CostEstimate(flops=flops, bytes_accessed=bytes_moved, transcendentals=exps)


def eight(ref, g):
    return ref[pl.ds(pl.multiple_of(g * 8, 8), 8), :]


def rows(block, i, nb):
    return [
        jnp.broadcast_to(block[i : i + 1, j * 128 : (j + 1) * 128], (8, 128)) for j in range(nb)
    ]


def tiles(ref, halves, nb):
    return [
        [ref[h * 8 : h * 8 + 8, j * 128 : j * 128 + 128] for h in range(halves)] for j in range(nb)
    ]


def state_kernel(delta_ref, x_ref, bias_ref, a_ref, b_ref, step_ref, fin_ref, u_ref):
    tokens, lanes = delta_ref.shape
    n = a_ref.shape[0]
    halves, nb = n // 8, lanes // 128
    v = delta_ref[...].astype(F32) + bias_ref[...]
    step = jnp.maximum(v, 0.0) + jnp.log1p(jnp.exp(-jnp.abs(v)))
    step_ref[...] = step
    u_ref[...] = step * x_ref[...].astype(F32)
    fin_ref[n : n + 8, :] = jnp.broadcast_to(jnp.sum(step, axis=0, keepdims=True), (8, lanes))
    a = tiles(a_ref, halves, nb)

    def body(g, carry):
        hs = list(carry)
        step8, u8 = eight(step_ref, g), eight(u_ref, g)
        for i in range(8):
            t = g * 8 + i
            b = [b_ref[pl.ds(pl.multiple_of(t * n + 8 * h, 8), 8), :] for h in range(halves)]
            ds, us = rows(step8, i, nb), rows(u8, i, nb)
            for j in range(nb):
                d, u = ds[j], us[j]
                for h in range(halves):
                    k = j * halves + h
                    hs[k] = jnp.exp2(d * a[j][h]) * hs[k] + u * b[h]
        return tuple(hs)

    zero = jnp.zeros((8, 128), F32)
    hs = lax.fori_loop(0, tokens // 8, body, (zero,) * (halves * nb))
    for j in range(nb):
        for h in range(halves):
            fin_ref[h * 8 : h * 8 + 8, j * 128 : j * 128 + 128] = hs[j * halves + h]


def fold_rows(parts, masks):
    for width, mask in zip((4, 2, 1), masks):
        count = len(parts) // 2
        merged = []
        for i in range(count):
            p, q = parts[i], parts[i + count]
            if width == 4:
                other = pltpu.roll(jnp.where(mask, q, p), 4, 0)
            else:
                other = jnp.where(mask, pltpu.roll(p, 8 - width, 0), pltpu.roll(q, width, 0))
            merged.append(jnp.where(mask, p, q) + other)
        parts = merged
    return parts[0]


def scan_kernel(
    step_ref, x_ref, gate_ref, skip_ref, a_ref, b_ref, c_ref, h_ref, out_ref, u_ref, y_ref
):
    tokens, lanes = step_ref.shape
    n = a_ref.shape[0]
    halves, nb = n // 8, lanes // 128
    u_ref[...] = step_ref[...] * x_ref[...].astype(F32)
    a = tiles(a_ref, halves, nb)
    start = tiles(h_ref, halves, nb)
    sub = lax.broadcasted_iota(jnp.int32, (8, 128), 0)
    masks = [(sub & w) == 0 for w in (4, 2, 1)]

    def body(g, carry):
        hs = list(carry)
        step8, u8 = eight(step_ref, g), eight(u_ref, g)
        sums = [[None] * 8 for _ in range(nb)]
        for i in range(8):
            t = g * 8 + i
            b = [b_ref[pl.ds(pl.multiple_of(t * n + 8 * h, 8), 8), :] for h in range(halves)]
            c = [c_ref[pl.ds(pl.multiple_of(t * n + 8 * h, 8), 8), :] for h in range(halves)]
            ds, us = rows(step8, i, nb), rows(u8, i, nb)
            for j in range(nb):
                d, u = ds[j], us[j]
                total = None
                for h in range(halves):
                    k = j * halves + h
                    hs[k] = jnp.exp2(d * a[j][h]) * hs[k] + u * b[h]
                    term = hs[k] * c[h]
                    total = term if total is None else total + term
                sums[j][i] = total
        for j in range(nb):
            y_ref[pl.ds(pl.multiple_of(g * 8, 8), 8), j * 128 : j * 128 + 128] = fold_rows(sums[j], masks)
        return tuple(hs)

    lax.fori_loop(0, tokens // 8, body, tuple(start[j][h] for j in range(nb) for h in range(halves)))
    x = x_ref[...].astype(F32)
    v = gate_ref[...].astype(F32)
    scanned = y_ref[...] + skip_ref[...] * x
    out_ref[...] = (scanned * (v / (1.0 + jnp.exp(-v)))).astype(BF16)


def scan_specs(tokens, n, lanes):
    wide = pl.BlockSpec((tokens, lanes), lambda i: (0, i))
    one = pl.BlockSpec((1, lanes), lambda i: (0, i))
    state = pl.BlockSpec((n, lanes), lambda i: (0, i))
    whole = pl.BlockSpec((tokens * n, 128), lambda i: (0, 0))
    return wide, one, state, whole


def local_state(delta, x, bias, a2, b_wide):
    tokens, width = delta.shape
    n = a2.shape[0]
    lanes = math.gcd(width, 512)
    wide, one, state, whole = scan_specs(tokens, n, lanes)
    return pl.pallas_call(
        state_kernel,
        grid=(width // lanes,),
        in_specs=[wide, wide, one, state, whole],
        out_specs=[wide, pl.BlockSpec((n + 8, lanes), lambda i: (0, i))],
        out_shape=[
            jax.ShapeDtypeStruct((tokens, width), F32),
            jax.ShapeDtypeStruct((n + 8, width), F32),
        ],
        scratch_shapes=[pltpu.VMEM((tokens, lanes), F32)],
        cost_estimate=cost(8 * tokens * width * n, 8 * tokens * width, tokens * width * n),
        name="local_state",
    )(delta, x, bias, a2, b_wide)


def gated_scan(step, x, gate, skip, a2, b_wide, c_wide, entering):
    tokens, width = step.shape
    n = a2.shape[0]
    lanes = math.gcd(width, 512)
    wide, one, state, whole = scan_specs(tokens, n, lanes)
    return pl.pallas_call(
        scan_kernel,
        grid=(width // lanes,),
        in_specs=[wide, wide, wide, one, state, whole, whole, state],
        out_specs=wide,
        out_shape=jax.ShapeDtypeStruct((tokens, width), BF16),
        scratch_shapes=[pltpu.VMEM((tokens, lanes), F32)] * 2,
        cost_estimate=cost(12 * tokens * width * n, 10 * tokens * width, tokens * width * n),
        name="gated_scan",
    )(step, x, gate, skip, a2, b_wide, c_wide, entering)


def out_kernel(idx_ref, x_ref, w_ref, send_ref, keep_ref):
    prod = jnp.dot(x_ref[...], w_ref[...], preferred_element_type=F32)
    sending = pl.program_id(0) < pl.num_programs(0) // 2

    @pl.when(sending)
    def _():
        send_ref[...] = prod.astype(BF16)

    @pl.when(jnp.logical_not(sending))
    def _():
        keep_ref[...] = prod


def project_blocks(gated, weight, blocks, bn):
    tokens, depth = gated.shape
    count = blocks.shape[0]
    half = count // 2
    return pl.pallas_call(
        out_kernel,
        grid_spec=pltpu.PrefetchScalarGridSpec(
            num_scalar_prefetch=1,
            grid=(count,),
            in_specs=[
                pl.BlockSpec((tokens, depth), lambda j, idx: (0, 0)),
                pl.BlockSpec((depth, bn), lambda j, idx: (0, idx[j])),
            ],
            out_specs=[
                pl.BlockSpec((tokens, bn), lambda j, idx: (0, jnp.minimum(j, half - 1))),
                pl.BlockSpec((tokens, bn), lambda j, idx: (0, jnp.maximum(j - half, 0))),
            ],
        ),
        out_shape=[
            jax.ShapeDtypeStruct((tokens, half * bn), BF16),
            jax.ShapeDtypeStruct((tokens, half * bn), F32),
        ],
        cost_estimate=cost(2 * tokens * depth * count * bn, 2 * depth * count * bn),
    )(blocks, gated, weight)


def qkv_kernel(flag_ref, *refs, groups, tokens):
    xs = refs[: 4 * groups]
    own_w, far_w, send_ref, keep_ref, near_ref, rest_ref = refs[4 * groups :]

    @pl.when(pl.program_id(0) == 0)
    def _():
        swap = flag_ref[0] == 1
        for a in range(groups):
            for half, dst in ((0, near_ref), (1, rest_ref)):
                own = xs[half * 2 * groups + a][...]
                other = xs[half * 2 * groups + groups + a][...]
                dst[a * tokens : (a + 1) * tokens, :] = jnp.where(swap, own, other)
                dst[(groups + a) * tokens : (groups + a + 1) * tokens, :] = jnp.where(
                    swap, other, own
                )

    prod = jnp.dot(near_ref[...], own_w[...], preferred_element_type=F32)
    prod = prod + jnp.dot(rest_ref[...], far_w[...], preferred_element_type=F32)
    half_rows = groups * tokens
    send_ref[...] = prod[:half_rows].astype(BF16)
    keep_ref[...] = prod[half_rows:]


def qkv_piece(flag, xs, own_w, far_w, first, width):
    tokens, rows = xs[0].shape
    groups = len(xs) // 4
    bn = math.gcd(width, 512)
    offset = first // bn
    total = groups * tokens

    def body(*refs):
        qkv_kernel(*refs, groups=groups, tokens=tokens)

    x_spec = pl.BlockSpec((tokens, rows), lambda j, f: (0, 0))
    w_spec = pl.BlockSpec((rows, bn), lambda j, f: (0, offset + j))
    o_spec = pl.BlockSpec((total, bn), lambda j, f: (0, j))
    return pl.pallas_call(
        body,
        grid_spec=pltpu.PrefetchScalarGridSpec(
            num_scalar_prefetch=1,
            grid=(width // bn,),
            in_specs=[x_spec] * len(xs) + [w_spec, w_spec],
            out_specs=[o_spec, o_spec],
            scratch_shapes=[pltpu.VMEM((2 * total, rows), BF16)] * 2,
        ),
        out_shape=[
            jax.ShapeDtypeStruct((total, width), BF16),
            jax.ShapeDtypeStruct((total, width), F32),
        ],
        cost_estimate=cost(8 * total * rows * width, 4 * rows * width + 6 * total * width),
    )(flag, *xs, own_w, far_w)


def dot_t(q, k):
    return lax.dot_general(q, k, (((1,), (1,)), ((), ())), preferred_element_type=F32)


def lane_tiles(v, op):
    out = v[:, :128]
    for i in range(1, v.shape[1] // 128):
        out = op(out, v[:, i * 128 : i * 128 + 128])
    return out


def attn_kernel(pos_ref, q_ref, k_ref, v_ref, k2_ref, v2_ref, *rest):
    o_ref, s_ref = rest[-2:]
    tokens = q_ref.shape[0]
    depth = k_ref.shape[0]
    scale = LOG2E / math.sqrt(HD)
    z, y = pos_ref[0], pos_ref[1]
    q = q_ref[...]
    r = lax.broadcasted_iota(jnp.int32, (tokens, tokens), 0)
    c = lax.broadcasted_iota(jnp.int32, (tokens, tokens), 1)
    blocks = []
    for j in range(depth):
        blocks.append((k_ref, v_ref, j, None if j == 0 else j <= z))
        blocks.append((k2_ref, v2_ref, j, y == 1 if j == 0 else j <= z))
    top = None
    for i, (keys, _, j, valid) in enumerate(blocks):
        s = dot_t(q, keys[j])
        if valid is None:
            s = jnp.where(c <= r, s, -1e30)
        s_ref[i] = s
        m = lane_tiles(s, jnp.maximum)
        if valid is not None:
            m = jnp.where(valid, m, -1e30)
        top = m if top is None else jnp.maximum(top, m)
    top = jnp.max(top, axis=1, keepdims=True) * scale
    total, acc = None, None
    for i, (_, vals, j, valid) in enumerate(blocks):
        shift = top if valid is None else top + jnp.where(valid, 0.0, 1e30)
        p = jnp.exp2(s_ref[i] * scale - shift)
        part = lane_tiles(p, jnp.add)
        prod = jnp.dot(p.astype(BF16), vals[j], preferred_element_type=F32)
        total = part if total is None else total + part
        acc = prod if acc is None else acc + prod
    o_ref[...] = (acc / jnp.sum(total, axis=1, keepdims=True)).astype(BF16)


def attend(pos, q, near_kv, far_kv, done, first_head, all_heads, kv_heads):
    tokens, width = q.shape
    heads = width // HD
    depth = near_kv.shape[0]

    def kv(h):
        return (first_head + h) * kv_heads // all_heads

    q_spec = pl.BlockSpec((tokens, HD), lambda h, p: (0, h))
    o_spec = pl.BlockSpec((tokens, HD), lambda h, p: (0, first_head + h))
    extra = [] if done is None else [done]
    k_spec = pl.BlockSpec((depth, tokens, HD), lambda h, p: (0, 0, kv(h)))
    v_spec = pl.BlockSpec((depth, tokens, HD), lambda h, p: (0, 0, kv_heads + kv(h)))
    return pl.pallas_call(
        attn_kernel,
        grid_spec=pltpu.PrefetchScalarGridSpec(
            num_scalar_prefetch=1,
            grid=(heads,),
            in_specs=[q_spec, k_spec, v_spec, k_spec, v_spec]
            + [pl.BlockSpec(memory_space=pl.ANY)] * len(extra),
            out_specs=o_spec,
            scratch_shapes=[pltpu.VMEM((2 * depth, tokens, tokens), F32)],
        ),
        out_shape=jax.ShapeDtypeStruct((tokens, all_heads * HD), BF16),
        input_output_aliases={6: 0} if extra else {},
        cost_estimate=cost(
            8 * tokens * tokens * depth * width, 4 * tokens * width, 2 * tokens * tokens * depth * heads
        ),
    )(pos, q, near_kv, near_kv, far_kv, far_kv, *extra)


def shards(
    mamba_in,
    gate_in,
    delta_in,
    step_bias,
    decay_log,
    input_map_state,
    state_out,
    skip_gain,
    out_weight,
    residual,
    norm_gain,
    query_weight,
    key_weight,
    value_weight,
):
    S, C = lax.axis_size("seq"), lax.axis_size("ch")
    s, c = lax.axis_index("seq"), lax.axis_index("ch")
    Z, G = S // 2, S // 4
    z, y, k = s // 2, s % 2, c % 2
    tokens, width = mamba_in.shape
    n = decay_log.shape[1]
    model = out_weight.shape[1]
    R = model // S

    def swap_y(v):
        return lax.ppermute(v, "seq", [(i, i ^ 1) for i in range(S)])

    def xor_z(v, d):
        return lax.ppermute(v, "seq", [(i, i ^ (2 * d)) for i in range(S)])

    def xor_c(v, d):
        return lax.ppermute(v, "ch", [(i, i ^ d) for i in range(C)])

    a2 = (-LOG2E) * jnp.exp(decay_log).T
    b_wide = jnp.broadcast_to(input_map_state.astype(F32).reshape(-1, 1), (tokens * n, 128))
    c_wide = jnp.broadcast_to(state_out.astype(F32).reshape(-1, 1), (tokens * n, 128))

    gain = lax.dynamic_update_slice_in_dim(jnp.zeros((model,), BF16), norm_gain, c * width, 0)
    d = 1
    while d < C:
        gain = gain + xor_c(gain, d)
        d *= 2
    gain = gain.astype(F32)

    step, final = local_state(delta_in, mamba_in, step_bias[None], a2, b_wide)

    def pack(f, t):
        high = t.astype(BF16)
        low = (t - high.astype(F32)).astype(BF16)
        wide = [v.reshape(n, width // n) for v in (high, low)]
        return jnp.concatenate([f.astype(BF16)] + wide, axis=1)

    def unpack(v):
        part = width // n
        high, low = v[:, width : width + part], v[:, width + part :]
        return v[:, :width].astype(F32), (high.astype(F32) + low.astype(F32)).reshape(1, width)

    f_own, t_own = final[:n], final[n : n + 1]
    pair = swap_y(pack(f_own, t_own))
    f_far, t_far = unpack(pair)
    lead = y == 0
    f_pair = jnp.where(lead, f_own, f_far) * jnp.exp2(
        jnp.where(lead, t_far, t_own) * a2
    ) + jnp.where(lead, f_far, f_own)
    both = pack(f_pair, t_own + t_far)
    earlier = []
    for j in range(1, Z):
        earlier.append(lax.ppermute(both, "seq", [(i, i + 2 * j) for i in range(S - 2 * j)]))
    entering = unpack(earlier[-1])[0]
    for e in earlier[-2::-1]:
        f, t = unpack(e)
        entering = entering * jnp.exp2(t * a2) + f
    entering = jnp.where(lead, entering, entering * jnp.exp2(t_far * a2) + f_far)

    q_heads = query_weight.shape[1] // HD
    all_heads = query_weight.shape[1] * C // HD
    group = all_heads // (key_weight.shape[1] // HD)
    kv_heads = max(1, q_heads // group)
    first = (c * q_heads // group) * HD
    kv_own = jnp.concatenate(
        [lax.dynamic_slice_in_dim(w, first, kv_heads * HD, 1) for w in (key_weight, value_weight)],
        axis=1,
    )
    kv_far = swap_y(kv_own)
    q_far = swap_y(query_weight)

    gated = gated_scan(
        step, mamba_in, gate_in, skip_gain[None], a2, b_wide, c_wide, entering
    )

    def move(blocks):
        own = []
        for a in range(G):
            perm = []
            for zi in range(Z):
                for yi in range(2):
                    for ci in range(C):
                        zo = 2 * ((zi // 2) ^ a) + ci % 2
                        perm.append(
                            ((2 * zi + yi) * C + ci, (2 * zo + yi) * C + ci - ci % 2 + zi % 2)
                        )
            own.append(lax.ppermute(blocks[a], ("seq", "ch"), perm))
        return own + [xor_c(v, 1) for v in own]

    moved = []
    if C == Z and G == 2:
        cx = c // 2
        bn = math.gcd(R, 1024)
        per = R // bn
        straight = cx == z // 2
        sums, mixed = jnp.zeros((tokens,), F32), []
        for half in (0, 1):
            side = y ^ half
            places = jnp.stack([cx, cx ^ 1])
            m = 2 * (2 * places[None, :] + jnp.stack([1 - k, k])[:, None]) + side
            ids = m[..., None] * per + jnp.arange(per, dtype=jnp.int32)
            send, keep = project_blocks(gated, out_weight, ids.reshape(-1).astype(jnp.int32), bn)
            if half:
                keep, *mixed = lax.optimization_barrier((keep, *mixed))
            total = keep + xor_c(send, 1).astype(F32)
            got = xor_c(total[:, R:].astype(BF16), 2)
            if half:
                got, _ = lax.optimization_barrier((got, scaled))
            rest = lax.dynamic_slice_in_dim(residual, side * R, R, 1).astype(F32)
            own = (total[:, :R] + got.astype(F32) + rest).astype(BF16)
            other = xor_c(own, 2)
            mixed.append(own)
            scaled = []
            for e, v in enumerate((own, other)):
                first_col = (2 * (2 * places[e] + k) + side) * R
                wide = v.astype(F32)
                sums = sums + jnp.sum(wide * wide, axis=1)
                g = lax.dynamic_slice_in_dim(gain, first_col, R, 0)
                scaled.append((wide * g[None]).astype(BF16))
            moved += move(
                [
                    jnp.where(straight, scaled[0], scaled[1]),
                    jnp.where(straight, scaled[1], scaled[0]),
                ],
            )
        sums = sums + xor_c(sums, 1)
        mamba_out = jnp.concatenate(
            [jnp.where(y == i, mixed[0], mixed[1]) for i in (0, 1)], axis=1
        )
    else:
        partial_terms = jnp.dot(gated, out_weight, preferred_element_type=F32)
        projected = lax.psum_scatter(partial_terms, "ch", scatter_dimension=1, tiled=True)
        mamba_out = (residual.astype(F32) + projected).astype(BF16)
        full = lax.all_gather(mamba_out, "ch", axis=1, tiled=True).astype(F32)
        sums = jnp.sum(full * full, axis=1)
        full = (full * gain[None]).astype(BF16)
        for half in (0, 1):
            cols = [(2 * (2 * ((z // 2) ^ a) + k) + (y ^ half)) * R for a in range(G)]
            moved += move([lax.dynamic_slice_in_dim(full, v, R, 1) for v in cols])
    inverse = lax.rsqrt(sums / model + 1e-06)[:, None]

    flag = ((k ^ (z % 2)).astype(jnp.int32))[None]

    def project(own_w, far_w, lo, size, last=None):
        send, keep = qkv_piece(flag, moved, own_w, far_w, lo, size)
        got = xor_z(send, 1)
        if last is not None:
            got, _ = lax.optimization_barrier((got, last[0]))
        got = got.astype(F32)
        parts = [
            keep[a * tokens : (a + 1) * tokens] + got[a * tokens : (a + 1) * tokens]
            for a in range(G)
        ]
        bit = G // 2
        while bit:
            out = jnp.concatenate([v.astype(BF16) for v in parts[bit:]], axis=0)
            got = xor_z(out, 2 * bit)
            if last is not None:
                got, _ = lax.optimization_barrier((got, last[1]))
            got = got.astype(F32)
            parts = [parts[i] + got[i * tokens : (i + 1) * tokens] for i in range(bit)]
            bit //= 2
        return out, (parts[0] * inverse).astype(BF16)

    last = project(kv_own, kv_far, 0, kv_own.shape[1])
    kv_rows = last[1]
    near, far = [kv_rows], []
    for _ in range(1, Z):
        near.append(lax.ppermute(near[-1], "seq", [(i, i + 2) for i in range(S - 2)]))
    for v in near:
        far.append(swap_y(v))
    near, far = jnp.stack(near), jnp.stack(far)
    pos = jnp.stack([z, y]).astype(jnp.int32)
    result = None
    q_width = query_weight.shape[1]
    pieces = math.gcd(Q_PIECES, q_width // HD)
    size = q_width // pieces
    for i in range(pieces):
        last = project(query_weight, q_far, i * size, size, last)
        q = last[1]
        result = attend(pos, q, near, far, result, i * size // HD, q_heads, kv_heads)
    return (mamba_out, result)


def solution(mesh):
    return jax.shard_map(
        shards,
        mesh=mesh,
        in_specs=(
            P("seq", "ch"),
            P("seq", "ch"),
            P("seq", "ch"),
            P("ch"),
            P("ch", None),
            P("seq", None),
            P("seq", None),
            P("ch"),
            P("ch", None),
            P("seq", "ch"),
            P("ch"),
            P("seq", "ch"),
            P("seq", None),
            P("seq", None),
        ),
        out_specs=(P("seq", "ch"), P("seq", "ch")),
        check_vma=False,
    )
```
